32 devices in a mesh: groups: 2 (over y), ctx: 4 (over z), heads: 2 (over x), sub: 2 (over core).
Axes of the slice: x: 2, y: 2, z: 4, core: 2. Of those that a mesh axis runs over, the one named last changes fastest.
Arguments:
- queries: bfloat16 [2048, 4096], P(('groups', 'ctx', 'sub'), 'heads'), parts along dimension 0, may hold values from -6 to 6
- keys: bfloat16 [2048, 1024], P(('groups', 'ctx'), 'heads'), parts along dimension 0, may hold values from -6 to 6
- values: bfloat16 [2048, 1024], P(('groups', 'ctx'), 'heads'), parts along dimension 0, may hold values from -6 to 6
- image_keys: bfloat16 [256, 1024], P(('groups', 'ctx', 'sub'), 'heads'), parts along dimension 0, may hold values from -6 to 6
- image_values: bfloat16 [256, 1024], P(('groups', 'ctx', 'sub'), 'heads'), parts along dimension 0, may hold values from -6 to 6
- image_lengths: int32 [16], P('groups'), parts along dimension 0, may hold values from 1 to 32, 128 in all
- token_images: int32 [2048], P('groups'), parts along dimension 0, may hold values from 0 to 8, as said below
Outputs:
- self_out: bfloat16 [2048, 4096], P(('groups', 'ctx', 'sub'), 'heads'), parts along dimension 0
- cross_out: bfloat16 [2048, 4096], P(('groups', 'ctx', 'sub'), 'heads'), parts along dimension 0
The draws below stay inside these ranges and needn't reach their ends.
There are 2 independent parts, one for each index of `groups`. The reference program is written for one: setup_inputs(seed, part) draws one part's arguments, and reference() takes and returns one part's arrays. A program takes and returns all parts, laid end to end along the dimension named above; each array names one. Nothing has to cross between parts.
Inputs may be any that keep to these rules, and one draw needn't show every extreme that they name: `token_images`: never falls along the sequence; the first token sees no image and the last sees all 8.
All inputs are finite; a program needn't handle non-finite values.
Results may differ from the reference program's by a relative error of at most 0.005.
Values may be sent and summed in bfloat16 or wider, within the bound.
No kernel may reach another device: no remote copies, remote signals or barrier semaphores. Data moves between devices by JAX's collectives and lax.ppermute only.
A program may use at most 128 MiB of HBM per device.

```python
import math
import jax
import jax.numpy as jnp
import numpy as np
from jax import lax

QH = 32
KVH = 8
HD = 128
NIMG = 8
LEN = 1024
NV = 128


def draw_queries(key, part):
    shape = (LEN, QH * HD)
    return jnp.clip(jax.random.normal(jax.random.fold_in(key, 1), shape, jnp.float32), -6.0, 6.0).astype(jnp.bfloat16)


def draw_keys(key, part):
    shape = (LEN, KVH * HD)
    return jnp.clip(jax.random.normal(jax.random.fold_in(key, 2), shape, jnp.float32), -6.0, 6.0).astype(jnp.bfloat16)


def draw_image_keys(key, part):
    shape = (NV, KVH * HD)
    return jnp.clip(jax.random.normal(jax.random.fold_in(key, 3), shape, jnp.float32), -6.0, 6.0).astype(jnp.bfloat16)


def draw_token_images(key, part):
    spacing = LEN // NIMG
    jitter = jax.random.randint(jax.random.fold_in(key, 4), (NIMG,), 0, LEN // (2 * NIMG))
    first_token = 1 + jnp.arange(NIMG, dtype=jnp.int32) * spacing + jitter
    tokens_here = jnp.arange(LEN, dtype=jnp.int32)
    return jnp.sum((tokens_here[:, None] >= first_token[None, :]).astype(jnp.int32), axis=1).astype(jnp.int32)


def shard_levels(stream_key, dims, cuts, least, high):
    level = 1.0
    for axis_at, blocks in cuts:
        draws = jax.random.uniform(jax.random.fold_in(jax.random.fold_in(stream_key, 6), axis_at), (blocks,), jnp.float32, least / len(cuts), high / len(cuts))
        level = level * jnp.repeat(jnp.exp(draws), dims[axis_at] // blocks).reshape((-1,) + (1,) * (len(dims) - 1 - axis_at))
    return level


def split_up(count, total, limit, lean):
    portions = [(1 << 20) // math.isqrt(standing ** lean) + 1 for standing in range(2, count + 1)]
    surplus, holding = total - limit - (count - 1), [1] * (count - 1)
    while surplus > 0:
        candidates = [i for i in range(count - 1) if holding[i] < limit]
        whole, left = sum([portions[i] for i in candidates]), surplus
        for i in candidates:
            extra = min(limit - holding[i], max(1, left * portions[i] // whole), surplus)
            holding[i] = holding[i] + extra
            surplus = surplus - extra
    return np.array([limit] + holding)


def uneven_parts(stream_key, count, total, limit, slope):
    if count == 2:
        one = jax.random.randint(stream_key, (), max(1, total - limit), min(limit, total - 1) + 1)
        return jnp.stack([one, total - one])
    sizes = jnp.asarray(split_up(count, total, limit, slope), jnp.int32)
    pairs = (count - 1) // 2
    donor, receiver = sizes[1:1 + 2 * pairs:2], sizes[2:2 + 2 * pairs:2]
    room = jnp.minimum(donor - 1, limit - receiver)
    moved = jax.random.randint(jax.random.fold_in(stream_key, 1), (pairs,), 0, 1 << 20) % (room + 1)
    sizes = sizes.at[1:1 + 2 * pairs:2].set(donor - moved).at[2:2 + 2 * pairs:2].set(receiver + moved)
    return sizes[jax.random.permutation(jax.random.fold_in(stream_key, 2), count)]


def gaussian(rng, dims, scale, bound, split=(), held_as=jnp.bfloat16):
    factor_of = shard_levels(rng, dims, split, -0.22, 0.18) if split else 1.0
    entries = jax.random.normal(rng, dims, jnp.float32) * scale * factor_of
    return jnp.minimum(jnp.maximum(entries, -bound), bound).astype(held_as)


def setup_inputs(seed: int = 0, part: int = 0) -> dict:
    seeds = jax.random.split(jax.random.key(seed), 8)
    part_keys = jax.random.split(jax.random.fold_in(seeds[7], part), 8)
    queries = draw_queries(jax.random.fold_in(jax.random.fold_in(seeds[7], part), 71), part)
    keys = draw_keys(jax.random.fold_in(jax.random.fold_in(seeds[7], part), 71), part)
    values = gaussian(part_keys[2], (LEN, KVH * HD), 1.0, 6.0, ((0, 4), (1, 2)))
    image_keys = draw_image_keys(jax.random.fold_in(jax.random.fold_in(seeds[7], part), 71), part)
    image_values = gaussian(part_keys[4], (NV, KVH * HD), 1.0, 6.0, ((0, 8), (1, 2)))
    image_lengths = uneven_parts(part_keys[5], NIMG, NV, NV // 4, 2).astype(jnp.int32)
    token_images = draw_token_images(jax.random.fold_in(jax.random.fold_in(seeds[7], part), 71), part)
    return {"queries": queries, "keys": keys, "values": values, "image_keys": image_keys, "image_values": image_values, "image_lengths": image_lengths, "token_images": token_images}


def attend_heads(queries, keys, values, allowed, has_image):
    score_scale = 1.0 / math.sqrt(HD)
    group_size = QH // KVH

    def one_head(head):
        query_cols = lax.dynamic_slice_in_dim(queries, head * HD, HD, 1)
        key_cols = lax.dynamic_slice_in_dim(keys, head // group_size * HD, HD, 1)
        value_cols = lax.dynamic_slice_in_dim(values, head // group_size * HD, HD, 1)
        scores = jnp.dot(query_cols, key_cols.T, preferred_element_type=jnp.float32) * score_scale
        scores = jnp.where(allowed, scores, -1e+30)
        row_max = lax.optimization_barrier(jnp.max(scores, axis=1, keepdims=True))
        weights = jnp.where(allowed, jnp.exp(scores - row_max), 0.0)
        row_sum = lax.optimization_barrier(jnp.sum(weights, axis=1))
        result = jnp.dot(weights.astype(jnp.bfloat16), value_cols, preferred_element_type=jnp.float32)
        safe_sum = jnp.where(has_image, row_sum, 1.0)
        result = jnp.where(has_image[:, None], result / safe_sum[:, None], 0.0)
        return result.astype(jnp.bfloat16)
    stacked = lax.map(one_head, jnp.arange(QH, dtype=jnp.int32))
    return stacked.transpose(1, 0, 2).reshape(queries.shape[0], QH * HD)

def reference(queries, keys, values, image_keys, image_values, image_lengths, token_images):
    positions = jnp.arange(LEN, dtype=jnp.int32)
    causal = positions[None, :] <= positions[:, None]
    everyone = jnp.ones((LEN,), dtype=bool)
    self_out = attend_heads(queries, keys, values, causal, everyone)
    image_index = jnp.arange(NIMG, dtype=jnp.int32)
    visible = lax.optimization_barrier(jnp.sum(jnp.where(image_index[None, :] < token_images[:, None], image_lengths[None, :], 0), axis=1)).astype(jnp.int32)
    image_pos = jnp.arange(NV, dtype=jnp.int32)
    seen = image_pos[None, :] < visible[:, None]
    cross_out = attend_heads(queries, image_keys, image_values, seen, visible > 0)
    return (self_out, cross_out)
```

```python
import functools
import math

import jax
import jax.numpy as jnp
from jax import lax
from jax.experimental import pallas as pl
from jax.experimental.pallas import tpu as pltpu
from jax.sharding import PartitionSpec as P

QH = 32
KVH = 8
HD = 128
NIMG = 8
GROUP = QH // KVH
LANES = 128
SCALE = math.log2(math.e) / math.sqrt(HD)
NEG = -1e30
FLOOR = -1e29


def params():
    return pltpu.CompilerParams(vmem_limit_bytes=24 << 20)


def cost(rows, keys, heads):
    pairs = rows * keys * heads
    return pl.CostEstimate(
        flops=4 * pairs * HD, transcendentals=pairs, bytes_accessed=2 * rows * heads * HD
    )


def widen(column, width):
    return jnp.tile(column, (1, width // LANES))


def head_queries(q_ref, head):
    first = head * GROUP * HD
    return jnp.concatenate(
        [q_ref[:, first + g * HD : first + (g + 1) * HD] for g in range(GROUP)], axis=0
    )


def raw_scores(query, key):
    return lax.dot_general(
        query, key, (((1,), (1,)), ((), ())), preferred_element_type=jnp.float32
    )


def lane_sums(weights):
    total = weights[:, :LANES]
    for first in range(LANES, weights.shape[1], LANES):
        total = total + weights[:, first : first + LANES]
    return total


def row_max(scores):
    return jnp.broadcast_to(
        jnp.max(scores, axis=1, keepdims=True), (scores.shape[0], LANES)
    )


def start_state(scores, value):
    top = jnp.maximum(row_max(scores), FLOOR)
    weights = jnp.exp2((scores - widen(top, scores.shape[1])) * SCALE)
    out = jnp.dot(weights.astype(jnp.bfloat16), value, preferred_element_type=jnp.float32)
    return top, lane_sums(weights), out


def next_state(state, scores, value):
    top, total, out = state
    new_top = jnp.maximum(row_max(scores), top)
    weights = jnp.exp2((scores - widen(new_top, scores.shape[1])) * SCALE)
    factor = jnp.exp2((top - new_top) * SCALE)
    more = jnp.dot(weights.astype(jnp.bfloat16), value, preferred_element_type=jnp.float32)
    return new_top, total * factor + lane_sums(weights), out * factor + more


def put_heads(out_ref, head, result):
    rows = out_ref.shape[0]
    first = head * GROUP * HD
    for g in range(GROUP):
        out_ref[:, first + g * HD : first + (g + 1) * HD] = result[
            g * rows : (g + 1) * rows
        ].astype(out_ref.dtype)


def use_blocks(q_ref, blocks, first_step, state_refs, heads):
    width = heads * HD
    place = lax.axis_index("ctx")
    for step, pair in enumerate(blocks, first_step):

        @pl.when(place >= step)
        def _(pair=pair):
            for head in range(heads):
                query = head_queries(q_ref, head)
                cols = slice(head * HD, (head + 1) * HD)
                value_cols = slice(width + head * HD, width + (head + 1) * HD)
                key = jnp.concatenate([ref[:, cols] for ref in pair], axis=0)
                value = jnp.concatenate([ref[:, value_cols] for ref in pair], axis=0)
                state = tuple(ref[head] for ref in state_refs)
                state = next_state(state, raw_scores(query, key), value)
                for ref, part in zip(state_refs, state):
                    ref[head] = part


def finish(state_refs, out_ref, heads):
    for head in range(heads):
        total = jnp.sum(state_refs[1][head], axis=1, keepdims=True)
        put_heads(out_ref, head, state_refs[2][head] / total)


def first_kernel(steps, heads, q_ref, key_ref, value_ref, image_ref, seen_ref, *refs):
    flat, refs = refs[: 2 * steps], refs[2 * steps :]
    cross_ref, *state_refs = refs
    rows = q_ref.shape[0]
    keys_here = key_ref.shape[0]
    width = heads * HD
    core = lax.axis_index("sub")
    place = lax.axis_index("ctx")
    places = lax.axis_size("ctx")
    cores = lax.axis_size("sub")
    shape = (GROUP * rows, keys_here)
    row = lax.broadcasted_iota(jnp.int32, shape, 0) % rows + core * rows
    allowed = lax.broadcasted_iota(jnp.int32, shape, 1) <= row
    images = image_ref.shape[0]
    piece_rows = images // (places * cores)
    shape = (GROUP * rows, images)
    column = lax.broadcasted_iota(jnp.int32, shape, 1)
    piece = column // piece_rows
    owner = ((piece % places) ^ place) * cores + ((piece // places) ^ core)
    position = owner * piece_rows + column % piece_rows
    seen = jnp.concatenate([seen_ref[...]] * GROUP, axis=0)
    visible = position < widen(seen, images)
    for head in range(heads):
        query = head_queries(q_ref, head)
        cols = slice(head * HD, (head + 1) * HD)
        scores = jnp.where(allowed, raw_scores(query, key_ref[:, cols]), NEG)
        state = start_state(scores, value_ref[:, cols])
        for ref, part in zip(state_refs, state):
            ref[head] = part
        value_cols = slice(width + head * HD, width + (head + 1) * HD)
        scores = jnp.where(visible, raw_scores(query, image_ref[:, cols]), NEG)
        _, total, out = start_state(scores, image_ref[:, value_cols])
        total = jnp.sum(total, axis=1, keepdims=True)
        put_heads(cross_ref, head, jnp.where(total > 0, out / jnp.where(total > 0, total, 1.0), 0.0))
    blocks = [flat[2 * i : 2 * i + 2] for i in range(steps)]
    use_blocks(q_ref, blocks, 1, state_refs, heads)


def last_kernel(first_step, steps, last, heads, q_ref, *refs):
    flat, refs = refs[: 2 * steps], refs[2 * steps :]
    state_in, refs = refs[:3], refs[3:]
    blocks = [flat[2 * i : 2 * i + 2] for i in range(steps)]
    if last:
        out_ref, *state_refs = refs
    else:
        state_refs = refs
    for source, target in zip(state_in, state_refs):
        target[...] = source[...]
    use_blocks(q_ref, blocks, first_step, state_refs, heads)
    if last:
        finish(state_refs, out_ref, heads)


def local(queries, keys, values, image_keys, image_values, image_lengths, token_images):
    place = lax.axis_index("ctx")
    core = lax.axis_index("sub")
    places = lax.axis_size("ctx")
    cores = lax.axis_size("sub")
    rows = queries.shape[0]
    heads = keys.shape[1] // HD
    part = keys.shape[0] // cores

    def mine(array):
        return lax.dynamic_slice_in_dim(array, core * part, part)

    def swap(array):
        return lax.ppermute(array, "sub", [(i, i ^ 1) for i in range(cores)])

    block = jnp.concatenate([mine(keys), mine(values)], axis=1)
    images = jnp.concatenate([image_keys, image_values], axis=1)
    blocks = []
    for step in range(1, places):
        pairs = [(i, i) for i in range(step - 1)]
        pairs += [(i, i + 1) for i in range(step - 1, places - 1)]
        pairs += [(places - 1, step - 1)]
        block = lax.ppermute(block, "ctx", pairs)
        blocks.append((block, swap(block)))
    far = 1
    while far < places:
        other = lax.ppermute(images, "ctx", [(i, i ^ far) for i in range(places)])
        images = jnp.concatenate([images, other], axis=0)
        far *= 2
    images = jnp.concatenate([images, swap(images)], axis=0)

    first_row = (place * cores + core) * rows
    images_seen = lax.dynamic_slice_in_dim(token_images, first_row, rows)
    index = jnp.arange(NIMG, dtype=jnp.int32)
    visible = jnp.sum(
        jnp.where(index[None, :] < images_seen[:, None], image_lengths[None, :], 0), axis=1
    )
    seen = jnp.broadcast_to(visible[:, None], (rows, LANES)).astype(jnp.int32)

    tall = GROUP * rows
    state_shapes = tuple(
        jax.ShapeDtypeStruct((heads, tall, n), jnp.float32) for n in (LANES, LANES, HD)
    )
    result = jax.ShapeDtypeStruct(queries.shape, queries.dtype)
    vmem = pl.BlockSpec(memory_space=pltpu.VMEM)
    before = places - 2
    now = min(2, before)
    cross_out, *state = pl.pallas_call(
        functools.partial(first_kernel, now, heads),
        out_shape=(result, *state_shapes),
        in_specs=[vmem] * (5 + 2 * now),
        out_specs=[vmem] * 4,
        compiler_params=params(),
        cost_estimate=cost(rows, keys.shape[0] * (now + 1), heads * GROUP),
        name="first",
    )(queries, keys, values, images, seen, *[x for pair in blocks[:now] for x in pair])
    done = now
    while done < places - 1:
        now = min(2, before - done) if done < before else 1
        last = done + now == places - 1
        flat = [x for pair in blocks[done : done + now] for x in pair]
        outs = pl.pallas_call(
            functools.partial(last_kernel, done + 1, now, last, heads),
            out_shape=((result,) if last else state_shapes),
            in_specs=[vmem] * (4 + 2 * now),
            out_specs=[vmem] * (1 if last else 3),
            scratch_shapes=[pltpu.VMEM(s.shape, s.dtype) for s in state_shapes] if last else [],
            compiler_params=params(),
            cost_estimate=cost(rows, keys.shape[0] * now, heads * GROUP),
            name="last" if last else "more",
        )(queries, *flat, *state)
        if last:
            self_out = outs[0]
        else:
            state = outs
        done += now
    return self_out, cross_out


def solution(mesh):
    in_specs = (
        P(("groups", "ctx", "sub"), "heads"),
        P(("groups", "ctx"), "heads"),
        P(("groups", "ctx"), "heads"),
        P(("groups", "ctx", "sub"), "heads"),
        P(("groups", "ctx", "sub"), "heads"),
        P("groups"),
        P("groups"),
    )
    out_specs = (P(("groups", "ctx", "sub"), "heads"), P(("groups", "ctx", "sub"), "heads"))
    return jax.shard_map(local, mesh=mesh, in_specs=in_specs, out_specs=out_specs, check_vma=False)
```
